256 devices in a mesh: wide: 16 (over x, y), perm: 16 (over z, core).
Axes of the slice: x: 4, y: 4, z: 8, core: 2. Of those that a mesh axis runs over, the one named last changes fastest.
Arguments:
- amplitudes: bfloat16 [64, 2048, 2048], P('wide', 'perm'), may hold values from -6 to 6
- integrals: bfloat16 [2048, 2048], P('perm'), may hold values from -0.125 to 0.125
- coupling: float32 [64, 9], replicated, may hold values from -2 to 2
- pair_energy: float32 [64], P('wide'), may hold values from -2 to -0.5
- virtual_energy: float32 [2048], replicated, may hold values from 0.5 to 3
- tile_sizes: int32 [16], replicated, may hold values from 64 to 128, as said below
- blocks: int32 [64, 16, 16], P('wide'), may hold values 0 or 1
Outputs:
- update: bfloat16 [64, 2048, 2048], P('wide', 'perm')
The draws below stay inside these ranges and needn't reach their ends.
Inputs may be any that keep to these rules, and one draw needn't show every extreme that they name: `tile_sizes`: some tile has 128 live slots and some tile 128 // 2.
All inputs are finite; a program needn't handle non-finite values. No bound on the sum of `blocks` on one device may be relied on, other than what follows from the above.
Results may differ from the reference program's by a relative error of at most 0.0058.
Values may be sent and summed in bfloat16 or wider, within the bound.
No kernel may reach another device: no remote copies, remote signals or barrier semaphores. Data moves between devices by JAX's collectives and lax.ppermute only.
A program may use at most 128 MiB of HBM per device.

```python
import jax
import jax.numpy as jnp
from jax import lax

NV = 2048
TS = 128
BAND = 4
NT = 16
P_SIZE = 64


def draw_tile_sizes(key, part):
    first, second = jax.random.split(key)
    sizes = jax.random.randint(first, (NT,), TS // 2, TS + 1)
    order = jax.random.permutation(second, NT)
    sizes = sizes.at[order[0]].set(TS).at[order[1]].set(TS // 2)
    return sizes.astype(jnp.int32)


def set_ends(result, own_key, low, high):
    place = [jax.random.randint(jax.random.fold_in(own_key, axis), (), 0, length) for axis, length in enumerate(result.shape)]
    widest = result.shape.index(max(result.shape))
    neighbour = place[:widest] + [(place[widest] + 1) % result.shape[widest]] + place[widest + 1:]
    return result.at[tuple(place)].set(low).at[tuple(neighbour)].set(high)


def level_of(rng, extent, pieces, low, largest):
    loudness = 1.0
    for position, blocks in pieces:
        heights = jax.random.uniform(jax.random.fold_in(jax.random.fold_in(rng, 6), position), (blocks,), jnp.float32, low / len(pieces), largest / len(pieces))
        loudness = loudness * jnp.repeat(jnp.exp(heights), extent[position] // blocks).reshape((-1,) + (1,) * (len(extent) - 1 - position))
    return loudness


def normal_values(key, dims, scale, bound, shards=(), held_as=jnp.bfloat16):
    entries = scale * jax.random.normal(key, dims, jnp.float32)
    if shards:
        entries = entries * level_of(key, dims, shards, -0.22, 0.18)
    return jnp.clip(entries, -bound, bound).astype(held_as)


def setup_inputs(seed: int = 0) -> dict:
    key_of = jax.random.split(jax.random.key(seed), 8)
    amplitudes = normal_values(key_of[0], (P_SIZE, NV, NV), 1.0, 6.0, ((0, 16), (1, 16)))
    integrals = normal_values(key_of[1], (NV, NV), NV ** -0.5, 0.125, ((0, 16),))
    coupling = normal_values(key_of[2], (P_SIZE, 2 * BAND + 1), 0.35, 2.0, (), jnp.float32)
    pair_energy = jnp.clip(-2.0 + 1.5 * jax.random.uniform(key_of[3], (P_SIZE,), jnp.float32) ** level_of(key_of[3], (P_SIZE,), ((0, 16),), -0.2, 0.2), -2.0, -0.5)
    virtual_energy = jnp.clip(jax.random.uniform(key_of[4], (NV,), jnp.float32, 0.5, 3.0), 0.5, 3.0)
    tile_sizes = draw_tile_sizes(jax.random.fold_in(key_of[7], 71), 0)
    blocks = set_ends((jax.random.randint(key_of[6], (P_SIZE, NT, NT), 0, 3) < 2).astype(jnp.int32), jax.random.fold_in(key_of[6], 1), 0, 1)
    return {"amplitudes": amplitudes, "integrals": integrals, "coupling": coupling, "pair_energy": pair_energy, "virtual_energy": virtual_energy, "tile_sizes": tile_sizes, "blocks": blocks}


def reference(amplitudes, integrals, coupling, pair_energy, virtual_energy, tile_sizes, blocks):
    total_pairs = amplitudes.shape[0]
    width = amplitudes.shape[1]
    tile_count = tile_sizes.shape[0]
    slot_size = width // tile_count
    reach = (coupling.shape[1] - 1) // 2
    live_all = (jnp.arange(slot_size, dtype=jnp.int32)[None, :] < tile_sizes[:, None]).reshape(width).astype(jnp.float32)

    def one_pair(index):
        mixed = jnp.zeros((width, width), jnp.float32)
        for offset in range(2 * reach + 1):
            source = index + offset - reach
            valid = (source >= 0) & (source < total_pairs)
            clipped = jnp.clip(source, 0, total_pairs - 1).astype(jnp.int32)
            slab = lax.dynamic_index_in_dim(amplitudes, clipped, 0, keepdims=False).astype(jnp.float32)
            weight = jnp.where(valid, coupling[index, offset], jnp.float32(0.0))
            mixed = mixed + weight * slab
        cycle = jnp.dot(mixed.astype(jnp.bfloat16), integrals, preferred_element_type=jnp.float32).astype(jnp.bfloat16)
        cycle = lax.optimization_barrier(cycle)
        cycle_wide = cycle.astype(jnp.float32)
        residual = cycle_wide + cycle_wide.T
        pattern = lax.dynamic_index_in_dim(blocks, index, 0, keepdims=False).astype(jnp.float32)
        pattern = jnp.repeat(jnp.repeat(pattern, slot_size, axis=0), slot_size, axis=1)
        mask = pattern * live_all[:, None] * live_all[None, :]
        denom = virtual_energy[:, None] + virtual_energy[None, :] - pair_energy[index]
        return (mask * (residual / denom)).astype(jnp.bfloat16)

    return lax.map(one_pair, jnp.arange(total_pairs, dtype=jnp.int32))
```

```python
import jax
import jax.numpy as jnp
from jax import lax
from jax.experimental import pallas as pl
from jax.experimental.pallas import tpu as pltpu
from jax.sharding import PartitionSpec as P


TILE = 128


def wide_shift(block, distance):
    size = lax.axis_size("wide")
    route = [(i, i + distance) for i in range(size) if 0 <= i + distance < size]
    return lax.ppermute(block, "wide", route)


def perm_shift(block, dz, dc):
    size = lax.axis_size("perm")
    chips = size // 2
    route = [(i, ((i // 2 + dz) % chips) * 2 + ((i % 2) ^ dc)) for i in range(size)]
    return lax.ppermute(block, "perm", route)


def mix_body(place_ref, coef_ref, before_ref, own_ref, after_ref, mixed_ref):
    pairs, rows, width = own_ref.shape
    taps = coef_ref.shape[1]
    step = 32
    for start in range(0, rows, step):
        source = [
            ref[p, start : start + step, :].astype(jnp.float32)
            for ref in (before_ref, own_ref, after_ref)
            for p in range(pairs)
        ]
        for p in range(pairs):
            total = coef_ref[p, 0] * source[p]
            for k in range(1, taps):
                total = total + coef_ref[p, k] * source[p + k]
            mixed_ref[p, start : start + step, :] = total.astype(jnp.bfloat16)


def mix(place, coef, before, own, after):
    pairs, rows, width = own.shape
    tiles = width // TILE

    def moved(t, place_ref):
        chips = tiles // 2
        dz = lax.rem(t // 2 - place_ref[0] + chips, chips)
        dc = lax.rem(t + place_ref[1], 2)
        return (0, 0, dz * 2 + dc)

    spec = pl.BlockSpec((pairs, rows, TILE), lambda t, place_ref: (0, 0, t))
    return pl.pallas_call(
        mix_body,
        out_shape=jax.ShapeDtypeStruct((pairs, rows, width), jnp.bfloat16),
        grid_spec=pltpu.PrefetchScalarGridSpec(
            num_scalar_prefetch=1,
            grid=(tiles,),
            in_specs=[pl.BlockSpec(memory_space=pltpu.SMEM), spec, spec, spec],
            out_specs=pl.BlockSpec((pairs, rows, TILE), moved),
        ),
        cost_estimate=pl.CostEstimate(
            flops=18 * pairs * rows * width, bytes_accessed=8 * pairs * rows * width, transcendentals=0
        ),
        name="mix",
    )(place, coef, before, own, after)


def product_body(mixed_ref, *refs):
    pieces, out_ref = refs[:-1], refs[-1]
    pairs, rows, width = mixed_ref.shape
    weights = jnp.concatenate([piece[...] for piece in pieces], axis=0)
    left = mixed_ref[...].reshape(pairs * rows, width)
    result = jnp.dot(left, weights, preferred_element_type=jnp.float32).astype(jnp.bfloat16)
    for t in range(out_ref.shape[0]):
        out_ref[t] = result[:, t * TILE : (t + 1) * TILE].reshape(pairs, rows, TILE)


def product(mixed, pieces):
    pairs, rows, width = mixed.shape
    tiles = width // TILE
    group = 2
    return pl.pallas_call(
        product_body,
        out_shape=jax.ShapeDtypeStruct((tiles, pairs, rows, TILE), jnp.bfloat16),
        grid=(tiles // group,),
        in_specs=[pl.BlockSpec((pairs, rows, width), lambda t: (0, 0, 0))]
        + [pl.BlockSpec((piece.shape[0], group * TILE), lambda t: (0, t)) for piece in pieces],
        out_specs=pl.BlockSpec((group, pairs, rows, TILE), lambda t: (t, 0, 0, 0)),
        cost_estimate=pl.CostEstimate(
            flops=2 * pairs * rows * width * width,
            bytes_accessed=4 * pairs * rows * width + 2 * width * width,
            transcendentals=0,
        ),
        name="product",
    )(mixed, *pieces)


def scale_body(mine_ref, sizes_ref, pair_ref, block_ref, row_ref, column_ref, out_ref):
    t = pl.program_id(0)
    tiles, pairs = block_ref.shape
    shape = (TILE, TILE)
    live = (lax.broadcasted_iota(jnp.int32, shape, 0) < sizes_ref[mine_ref[0]]) & (
        lax.broadcasted_iota(jnp.int32, shape, 1) < sizes_ref[t]
    )
    energy = row_ref[...] + column_ref[0]
    for p in range(pairs):
        block = block_ref[t, p].astype(jnp.float32)
        out_ref[0, p] = jnp.where(live, block / (energy - pair_ref[p]), 0.0)


def scale(mine, sizes, pair_energy, block_row, energy_row, energy_all):
    tiles = sizes.shape[0]
    pairs = pair_energy.shape[0]
    smem = pl.BlockSpec(memory_space=pltpu.SMEM)
    return pl.pallas_call(
        scale_body,
        out_shape=jax.ShapeDtypeStruct((tiles, pairs, TILE, TILE), jnp.float32),
        grid=(tiles,),
        in_specs=[
            smem,
            smem,
            smem,
            smem,
            pl.BlockSpec((TILE, 1), lambda t: (0, 0)),
            pl.BlockSpec((1, 1, TILE), lambda t: (t, 0, 0)),
        ],
        out_specs=pl.BlockSpec((1, pairs, TILE, TILE), lambda t: (t, 0, 0, 0)),
        cost_estimate=pl.CostEstimate(
            flops=10 * tiles * pairs * TILE * TILE,
            bytes_accessed=4 * tiles * pairs * TILE * TILE,
            transcendentals=0,
        ),
        name="scale",
    )(mine, sizes, pair_energy, block_row, energy_row, energy_all)


def finish_body(factor_ref, cycle_ref, swapped_ref, out_ref):
    group, pairs = cycle_ref.shape[:2]
    for t in range(group):
        for p in range(pairs):
            turned = swapped_ref[t, p].T.astype(jnp.float32)
            residual = cycle_ref[t, p].astype(jnp.float32) + turned
            out_ref[p, :, t * TILE : (t + 1) * TILE] = (factor_ref[t, p] * residual).astype(jnp.bfloat16)


def finish(factor, cycle, swapped):
    tiles, pairs = cycle.shape[:2]
    group = 2
    spec = pl.BlockSpec((group, pairs, TILE, TILE), lambda t: (t, 0, 0, 0))
    return pl.pallas_call(
        finish_body,
        out_shape=jax.ShapeDtypeStruct((pairs, TILE, tiles * TILE), jnp.bfloat16),
        grid=(tiles // group,),
        in_specs=[spec, spec, spec],
        out_specs=pl.BlockSpec((pairs, TILE, group * TILE), lambda t: (0, 0, t)),
        cost_estimate=pl.CostEstimate(
            flops=3 * tiles * pairs * TILE * TILE,
            bytes_accessed=10 * tiles * pairs * TILE * TILE,
            transcendentals=0,
        ),
        name="finish",
    )(factor, cycle, swapped)


def gathered(integrals):
    rows = integrals.shape[0]
    half = rows // 2
    chips = lax.axis_size("perm") // 2
    own = [None] * chips
    own[0] = [integrals]
    ahead = behind = integrals
    for step in range(1, chips // 2):
        ahead = perm_shift(ahead, 1, 0)
        behind = perm_shift(behind, -1, 0)
        own[chips - step] = [ahead]
        own[step] = [behind]
    own[chips // 2] = [perm_shift(ahead[:half], 1, 0), perm_shift(behind[half:], -1, 0)]
    pieces = []
    for chip in own:
        pieces += chip
        pieces += [perm_shift(piece, 0, 1) for piece in chip]
    return pieces


def per_device(amplitudes, integrals, coupling, pair_energy, virtual_energy, tile_sizes, blocks):
    pairs, rows, width = amplitudes.shape
    tiles = tile_sizes.shape[0]
    wide_index = lax.axis_index("wide")
    perm_index = lax.axis_index("perm")
    place = jnp.stack([perm_index // 2, perm_index % 2]).astype(jnp.int32)
    coef = lax.dynamic_slice_in_dim(coupling, wide_index * pairs, pairs, 0)
    before = wide_shift(amplitudes, 1)
    after = wide_shift(amplitudes, -1)
    pieces = gathered(integrals)
    block_row = lax.dynamic_index_in_dim(blocks, perm_index, 1, keepdims=False).T
    energy_row = lax.dynamic_slice_in_dim(virtual_energy, perm_index * rows, rows, 0)[:, None]
    factor = scale(
        perm_index.reshape(1).astype(jnp.int32),
        tile_sizes,
        pair_energy,
        block_row,
        energy_row,
        virtual_energy.reshape(tiles, 1, TILE),
    )
    mixed = mix(place, coef, before, amplitudes, after)
    cycle = product(mixed, pieces)
    swapped = lax.all_to_all(cycle, "perm", split_axis=0, concat_axis=0, tiled=True)
    return finish(factor, cycle, swapped)


def solution(mesh):
    in_specs = (
        P("wide", "perm", None),
        P("perm", None),
        P(),
        P("wide"),
        P(),
        P(),
        P("wide", None, None),
    )
    out_specs = P("wide", "perm", None)
    return jax.shard_map(
        per_device, mesh=mesh, in_specs=in_specs, out_specs=out_specs, check_vma=False
    )
```

```python
import functools

import jax
import jax.numpy as jnp
from jax import lax
from jax.experimental import pallas as pl
from jax.experimental.pallas import tpu as pltpu
from jax.sharding import PartitionSpec as P


TILE = 128
PARTS = 2
STREAMS = 4
FAR_FIRST = (4, 3, 5, 2, 6, 1, 7)
FINISH = ((0, 4, 3, 5), (2, 6), (1, 7))


def wide_shift(block, distance):
    size = lax.axis_size("wide")
    route = [(i, i + distance) for i in range(size) if 0 <= i + distance < size]
    return lax.ppermute(block, "wide", route)


def core_swap(block):
    size = lax.axis_size("perm")
    return lax.ppermute(block, "perm", [(i, i ^ 1) for i in range(size)])


def mirrored(block, distance):
    size = lax.axis_size("perm")
    chips = size // 2
    route = []
    for i in range(size):
        z, core = divmod(i, 2)
        route.append((i, (z + (distance if core == 0 else -distance)) % chips * 2 + core))
    return lax.ppermute(block, "perm", route)


def place():
    index = lax.axis_index("perm")
    return index // 2, lax.rem(index, 2)


def steps_from(z, chips, turn=0):
    own, core = place()
    core = lax.rem(core + turn, 2)
    ahead = lax.rem(own - z + chips, chips)
    return jnp.where(core == 0, ahead, lax.rem(chips - ahead, chips))


def mix_body(coef_ref, before_ref, own_ref, after_ref, *mixed_refs):
    pairs, rows, width = own_ref.shape
    taps = coef_ref.shape[1]
    chips = width // TILE // 2
    step = 32

    def one_tile(t, carry):
        source = pl.ds(pl.multiple_of(t * TILE, TILE), TILE)
        targets = []
        for turn in range(2):
            dz = steps_from(t // 2, chips, turn)
            dc = lax.rem(t + place()[1] + turn, 2)
            targets.append(pl.ds(pl.multiple_of((dz * 2 + dc) * TILE, TILE), TILE))
        for start in range(0, rows, step):
            total = [None] * pairs
            for q in range(3 * pairs):
                ref = (before_ref, own_ref, after_ref)[q // pairs]
                value = ref[q % pairs, start : start + step, source].astype(jnp.float32)
                for p in range(pairs):
                    if 0 <= q - p < taps:
                        term = coef_ref[p, q - p] * value
                        total[p] = term if total[p] is None else total[p] + term
            for p in range(pairs):
                rounded = total[p].astype(jnp.bfloat16)
                for ref, target in zip(mixed_refs, targets):
                    ref[p, start : start + step, target] = rounded
        return carry

    lax.fori_loop(0, width // TILE, one_tile, 0)


def mix(which, coef, before, own, after):
    pairs, rows, width = own.shape
    rows = rows // PARTS
    step = 32
    smem = pl.BlockSpec(memory_space=pltpu.SMEM)
    skip = which * rows // step
    spec = pl.BlockSpec((pairs, step, width), lambda t: (0, skip + t, 0))
    return pl.pallas_call(
        mix_body,
        out_shape=[jax.ShapeDtypeStruct((pairs, rows, width), jnp.bfloat16)] * 2,
        grid=(rows // step,),
        in_specs=[smem, spec, spec, spec],
        out_specs=[pl.BlockSpec((pairs, step, width), lambda t: (0, t, 0))] * 2,
        cost_estimate=pl.CostEstimate(
            flops=18 * pairs * rows * width, bytes_accessed=8 * pairs * rows * width, transcendentals=0
        ),
        name="mix",
    )(coef, before, own, after)


def split_body(in_ref, *refs):
    kept_refs, given_ref = refs[:-1], refs[-1]
    depth = kept_refs[0].shape[0]
    _, core = place()
    for z in range(given_ref.shape[1] // TILE):
        target = pl.ds(z * TILE, TILE)
        mine = pl.ds(pl.multiple_of((2 * z + core) * TILE, TILE), TILE)
        other = pl.ds(pl.multiple_of((2 * z + 1 - core) * TILE, TILE), TILE)
        given_ref[:, target] = in_ref[:, other]
        for i, ref in enumerate(kept_refs):
            ref[:, target] = in_ref[i * depth : (i + 1) * depth, mine]


def split(integrals):
    rows, width = integrals.shape
    depth = 2 * rows // STREAMS
    count = rows // depth
    vmem = pl.BlockSpec(memory_space=pltpu.VMEM)
    return pl.pallas_call(
        split_body,
        out_shape=[jax.ShapeDtypeStruct((depth, width // 2), jnp.bfloat16)] * count
        + [jax.ShapeDtypeStruct((rows, width // 2), jnp.bfloat16)],
        in_specs=[vmem],
        out_specs=[vmem] * (count + 1),
        cost_estimate=pl.CostEstimate(flops=0, bytes_accessed=4 * rows * width, transcendentals=0),
        name="split",
    )(integrals)


def product_body(count, chips, *refs):
    mixed_refs, pieces, outs = refs[:2], refs[2 : 2 + count], refs[-2 - chips :]
    own_refs, sent_refs = outs[:2], outs[2:]
    pairs, rows, width = mixed_refs[0].shape
    halves = sent_refs[0].shape[1]
    weights = jnp.concatenate([piece[...] for piece in pieces], axis=0)
    left = jnp.concatenate([ref[...].reshape(pairs * rows, width) for ref in mixed_refs], axis=0)
    result = jnp.dot(left, weights, preferred_element_type=jnp.float32).astype(jnp.bfloat16)
    for c in range(2):
        part = result[c * pairs * rows : (c + 1) * pairs * rows]
        own_refs[c][...] = part.reshape(pairs, rows, part.shape[1])
    turned = result.T
    group = result.shape[1] // TILE
    for i in range(group):
        z = pl.program_id(0) * group + i
        slot = lax.rem(chips - steps_from(z, chips), chips)

        def store(ref, i=i):
            for c in range(2):
                for h in range(halves):
                    start = (c * halves + h) * TILE
                    ref[c, h] = turned[i * TILE : (i + 1) * TILE, start : start + TILE]

        for d in range(chips):
            pl.when(slot == d)(functools.partial(store, sent_refs[d]))


def product(which, mixed, other, pieces, targets):
    pairs, rows, width = mixed.shape
    columns = pieces[0].shape[1]
    chips = columns // TILE
    wide = 2 * TILE
    halves = pairs * rows // TILE
    own = jax.ShapeDtypeStruct((pairs, PARTS * rows, columns), jnp.bfloat16)
    own_spec = pl.BlockSpec((pairs, rows, wide), lambda t: (0, which, t))
    sent_shape = (2, halves, TILE, TILE)
    first = 2 + len(pieces)
    return pl.pallas_call(
        functools.partial(product_body, len(pieces), chips),
        out_shape=[own, own] + [jax.ShapeDtypeStruct(sent_shape, jnp.bfloat16)] * chips,
        grid=(columns // wide,),
        in_specs=[pl.BlockSpec((pairs, rows, width), lambda t: (0, 0, 0))] * 2
        + [pl.BlockSpec((piece.shape[0], wide), lambda t: (0, t)) for piece in pieces]
        + [pl.BlockSpec(memory_space=pl.ANY)] * len(targets),
        out_specs=[own_spec, own_spec] + [pl.BlockSpec(sent_shape, lambda t: (0, 0, 0, 0))] * chips,
        input_output_aliases={first + i: i for i in range(len(targets))},
        cost_estimate=pl.CostEstimate(
            flops=4 * pairs * rows * width * columns,
            bytes_accessed=4 * pairs * rows * (width + columns) + 2 * width * columns,
            transcendentals=0,
        ),
        name="product",
    )(mixed, other, *pieces, *targets)


def finish_body(count, source_ref, sizes_ref, pair_ref, block_ref, row_ref, column_ref, own_ref, other_ref, *refs):
    swapped_refs, out_ref = refs[: PARTS * count], refs[-1]
    pairs = out_ref.shape[0]
    share = pairs // swapped_refs[0].shape[1]
    inner = TILE // share
    own, core = place()
    shape = (TILE, TILE)
    row_live = lax.broadcasted_iota(jnp.int32, shape, 0) < sizes_ref[own * 2 + core]
    lane = lax.broadcasted_iota(jnp.int32, shape, 1)
    source = source_ref[pl.program_id(0)]

    def one(d):
        for rel, mine_ref in enumerate((own_ref, other_ref)):
            half = lax.rem(core + rel, 2)
            tile = source * 2 + half
            target = pl.ds(pl.multiple_of(half * TILE, TILE), TILE)
            live = row_live & (lane < sizes_ref[tile])
            energy = row_ref[...] + column_ref[half]
            for p in range(pairs):
                start = p % share * inner
                theirs = jnp.concatenate(
                    [
                        swapped_refs[r * count + d][rel, p // share, :, start : start + inner]
                        for r in range(PARTS)
                    ],
                    axis=1,
                )
                residual = mine_ref[p].astype(jnp.float32) + theirs.astype(jnp.float32)
                block = jnp.where(live, block_ref[tile, p].astype(jnp.float32), 0.0)
                scaled = residual * pl.reciprocal(energy - pair_ref[p])
                out_ref[p, :, target] = (block * scaled).astype(jnp.bfloat16)

    for d in range(count):
        pl.when(pl.program_id(0) == d)(functools.partial(one, d))


def finish(sources, sizes, pair_energy, block_row, energy_row, energy_all, own, other, swapped, target):
    pairs, rows, columns = own.shape
    count = len(swapped) // PARTS
    smem = pl.BlockSpec(memory_space=pltpu.SMEM)
    own_spec = pl.BlockSpec((pairs, rows, TILE), lambda t, source: (0, 0, source[t]))
    before = 8 + len(swapped)
    return pl.pallas_call(
        functools.partial(finish_body, count),
        out_shape=jax.ShapeDtypeStruct((pairs, rows, 2 * columns), jnp.bfloat16),
        grid_spec=pltpu.PrefetchScalarGridSpec(
            num_scalar_prefetch=1,
            grid=(count,),
            in_specs=[
                smem,
                smem,
                smem,
                pl.BlockSpec((rows, 1), lambda t, source: (0, 0)),
                pl.BlockSpec((2, 1, TILE), lambda t, source: (source[t], 0, 0)),
                own_spec,
                own_spec,
            ]
            + [pl.BlockSpec(block.shape, lambda t, source: (0, 0, 0, 0)) for block in swapped]
            + ([] if target is None else [pl.BlockSpec(memory_space=pl.ANY)]),
            out_specs=pl.BlockSpec((pairs, rows, 2 * TILE), lambda t, source: (0, 0, source[t])),
        ),
        input_output_aliases={} if target is None else {before: 0},
        cost_estimate=pl.CostEstimate(
            flops=20 * count * pairs * rows * TILE,
            bytes_accessed=12 * count * pairs * rows * TILE,
            transcendentals=0,
        ),
        name="finish",
    )(
        sources,
        sizes,
        pair_energy,
        block_row,
        energy_row,
        energy_all,
        own,
        other,
        *swapped,
        *([] if target is None else [target]),
    )


def per_device(amplitudes, integrals, coupling, pair_energy, virtual_energy, tile_sizes, blocks):
    pairs, rows, _ = amplitudes.shape
    tiles = tile_sizes.shape[0]
    chips = tiles // 2
    wide_index = lax.axis_index("wide")
    perm_index = lax.axis_index("perm")
    coef = lax.dynamic_slice_in_dim(coupling, wide_index * pairs, pairs, 0)
    before = wide_shift(amplitudes, 1)
    after = wide_shift(amplitudes, -1)
    *kept_columns, given_columns = split(integrals)
    taken_columns = core_swap(given_columns)
    depth = 2 * rows // STREAMS
    moving = kept_columns + [taken_columns[start : start + depth] for start in range(0, rows, depth)]
    pieces = list(moving)
    for _ in range(1, chips):
        for i in range(STREAMS):
            moving[i] = mirrored(moving[i], 1)
        pieces += moving
    mixed, other = [], []
    for r in range(PARTS):
        kept_rows, given_rows = mix(r, coef, before, amplitudes, after)
        mixed.append(kept_rows)
        other.append(core_swap(given_rows))
    own, arrived = [], []
    for r in range(PARTS):
        kept, given, *sent = product(r, mixed[r], other[r], pieces, own)
        own = [kept, given]
        got = {0: sent[0]}
        for d in FAR_FIRST:
            got[d] = mirrored(sent[d], d)
        arrived.append(got)
    returned = core_swap(own[1])
    block_row = lax.dynamic_index_in_dim(blocks, perm_index, 1, keepdims=False).T
    energy_row = lax.dynamic_slice_in_dim(virtual_energy, perm_index * rows, rows, 0)[:, None]
    update = None
    for group in FINISH:
        back = jnp.array(group, jnp.int32)
        sources = (perm_index // 2 + jnp.where(perm_index % 2 == 0, chips - back, back)) % chips
        ready = [arrived[r][d] for r in range(PARTS) for d in group]
        update = finish(
            sources.astype(jnp.int32),
            tile_sizes,
            pair_energy,
            block_row,
            energy_row,
            virtual_energy.reshape(tiles, 1, TILE),
            own[0],
            returned,
            ready,
            update,
        )
    return update


def solution(mesh):
    in_specs = (
        P("wide", "perm", None),
        P("perm", None),
        P(),
        P("wide"),
        P(),
        P(),
        P("wide", None, None),
    )
    out_specs = P("wide", "perm", None)

    return jax.shard_map(
        per_device, mesh=mesh, in_specs=in_specs, out_specs=out_specs, check_vma=False
    )
```

```python
import functools

import jax
import jax.numpy as jnp
from jax import lax
from jax.experimental import pallas as pl
from jax.experimental.pallas import tpu as pltpu
from jax.sharding import PartitionSpec as P


TILE = 128
PARTS = 2
STREAMS = 4
EARLY = (3, 4)
LATE = (5, 2, 6, 1, 7)
FINISH = ((0, 4, 3, 5), (2, 6, 1, 7))


def wide_shift(block, distance):
    size = lax.axis_size("wide")
    route = [(i, i + distance) for i in range(size) if 0 <= i + distance < size]
    return lax.ppermute(block, "wide", route)


def core_swap(block):
    size = lax.axis_size("perm")
    return lax.ppermute(block, "perm", [(i, i ^ 1) for i in range(size)])


def mirrored(block, distance):
    size = lax.axis_size("perm")
    chips = size // 2
    route = []
    for i in range(size):
        z, core = divmod(i, 2)
        route.append((i, (z + (distance if core == 0 else -distance)) % chips * 2 + core))
    return lax.ppermute(block, "perm", route)


def place():
    index = lax.axis_index("perm")
    return index // 2, lax.rem(index, 2)


def steps_from(z, chips, turn=0):
    own, core = place()
    core = lax.rem(core + turn, 2)
    ahead = lax.rem(own - z + chips, chips)
    return jnp.where(core == 0, ahead, lax.rem(chips - ahead, chips))


def mix_body(coef_ref, before_ref, own_ref, after_ref, *mixed_refs):
    pairs, rows, width = own_ref.shape
    taps = coef_ref.shape[1]
    chips = width // TILE // 2
    step = 32

    def one_tile(t, carry):
        source = pl.ds(pl.multiple_of(t * TILE, TILE), TILE)
        targets = []
        for turn in range(2):
            dz = steps_from(t // 2, chips, turn)
            dc = lax.rem(t + place()[1] + turn, 2)
            targets.append(pl.ds(pl.multiple_of((dz * 2 + dc) * TILE, TILE), TILE))
        for start in range(0, rows, step):
            total = [None] * pairs
            for q in range(3 * pairs):
                ref = (before_ref, own_ref, after_ref)[q // pairs]
                value = ref[q % pairs, start : start + step, source].astype(jnp.float32)
                for p in range(pairs):
                    if 0 <= q - p < taps:
                        term = coef_ref[p, q - p] * value
                        total[p] = term if total[p] is None else total[p] + term
            for p in range(pairs):
                rounded = total[p].astype(jnp.bfloat16)
                for ref, target in zip(mixed_refs, targets):
                    ref[p, start : start + step, target] = rounded
        return carry

    lax.fori_loop(0, width // TILE, one_tile, 0)


def mix(which, coef, before, own, after):
    pairs, rows, width = own.shape
    rows = rows // PARTS
    step = 32
    smem = pl.BlockSpec(memory_space=pltpu.SMEM)
    skip = which * rows // step
    spec = pl.BlockSpec((pairs, step, width), lambda t: (0, skip + t, 0))
    return pl.pallas_call(
        mix_body,
        out_shape=[jax.ShapeDtypeStruct((pairs, rows, width), jnp.bfloat16)] * 2,
        grid=(rows // step,),
        in_specs=[smem, spec, spec, spec],
        out_specs=[pl.BlockSpec((pairs, step, width), lambda t: (0, t, 0))] * 2,
        cost_estimate=pl.CostEstimate(
            flops=18 * pairs * rows * width, bytes_accessed=8 * pairs * rows * width, transcendentals=0
        ),
        name="mix",
    )(coef, before, own, after)


def split_body(in_ref, *refs):
    kept_refs, given_ref = refs[:-1], refs[-1]
    depth = kept_refs[0].shape[0]
    _, core = place()
    for z in range(given_ref.shape[1] // TILE):
        target = pl.ds(z * TILE, TILE)
        mine = pl.ds(pl.multiple_of((2 * z + core) * TILE, TILE), TILE)
        other = pl.ds(pl.multiple_of((2 * z + 1 - core) * TILE, TILE), TILE)
        given_ref[:, target] = in_ref[:, other]
        for i, ref in enumerate(kept_refs):
            ref[:, target] = in_ref[i * depth : (i + 1) * depth, mine]


def split(integrals):
    rows, width = integrals.shape
    depth = 2 * rows // STREAMS
    count = rows // depth
    vmem = pl.BlockSpec(memory_space=pltpu.VMEM)
    return pl.pallas_call(
        split_body,
        out_shape=[jax.ShapeDtypeStruct((depth, width // 2), jnp.bfloat16)] * count
        + [jax.ShapeDtypeStruct((rows, width // 2), jnp.bfloat16)],
        in_specs=[vmem],
        out_specs=[vmem] * (count + 1),
        cost_estimate=pl.CostEstimate(flops=0, bytes_accessed=4 * rows * width, transcendentals=0),
        name="split",
    )(integrals)


def product_body(count, chips, *refs):
    mixed_refs, pieces, outs = refs[:2], refs[2 : 2 + count], refs[-2 - chips :]
    own_refs, sent_refs = outs[:2], outs[2:]
    pairs, rows, width = mixed_refs[0].shape
    halves = sent_refs[0].shape[2]
    weights = jnp.concatenate([piece[...] for piece in pieces], axis=0)
    left = jnp.concatenate([ref[...].reshape(pairs * rows, width) for ref in mixed_refs], axis=0)
    result = jnp.dot(left, weights, preferred_element_type=jnp.float32).astype(jnp.bfloat16)
    for c in range(2):
        part = result[c * pairs * rows : (c + 1) * pairs * rows]
        own_refs[c][...] = part.reshape(pairs, rows, part.shape[1])
    turned = result.T
    group = result.shape[1] // TILE
    for i in range(group):
        z = pl.program_id(0) * group + i
        slot = lax.rem(chips - steps_from(z, chips), chips)

        def store(ref, i=i):
            for c in range(2):
                for h in range(halves):
                    start = (c * halves + h) * TILE
                    ref[0, c, h] = turned[i * TILE : (i + 1) * TILE, start : start + TILE]

        for d in range(chips):
            pl.when(slot == d)(functools.partial(store, sent_refs[d]))


def product(which, mixed, other, pieces, own_targets, sent_targets):
    pairs, rows, width = mixed.shape
    columns = pieces[0].shape[1]
    chips = columns // TILE
    wide = 2 * TILE
    halves = pairs * rows // TILE
    own = jax.ShapeDtypeStruct((pairs, PARTS * rows, columns), jnp.bfloat16)
    own_spec = pl.BlockSpec((pairs, rows, wide), lambda t: (0, which, t))
    inner = (2, halves, TILE, TILE)
    sent_shapes, sent_specs = [], []
    targets = list(own_targets)
    aliases = {2 + len(pieces) + i: i for i in range(len(targets))}
    for d in range(chips):
        apart = d in EARLY
        sent_shapes.append(jax.ShapeDtypeStruct((1 if apart else PARTS,) + inner, jnp.bfloat16))
        at = 0 if apart else which
        sent_specs.append(pl.BlockSpec((1,) + inner, lambda t, at=at: (at, 0, 0, 0, 0)))
        if sent_targets and not apart:
            aliases[2 + len(pieces) + len(targets)] = 2 + d
            targets.append(sent_targets[d])
    return pl.pallas_call(
        functools.partial(product_body, len(pieces), chips),
        out_shape=[own, own] + sent_shapes,
        grid=(columns // wide,),
        in_specs=[pl.BlockSpec((pairs, rows, width), lambda t: (0, 0, 0))] * 2
        + [pl.BlockSpec((piece.shape[0], wide), lambda t: (0, t)) for piece in pieces]
        + [pl.BlockSpec(memory_space=pl.ANY)] * len(targets),
        out_specs=[own_spec, own_spec] + sent_specs,
        input_output_aliases=aliases,
        cost_estimate=pl.CostEstimate(
            flops=4 * pairs * rows * width * columns,
            bytes_accessed=4 * pairs * rows * (width + columns) + 2 * width * columns,
            transcendentals=0,
        ),
        name="product",
    )(mixed, other, *pieces, *targets)


def finish_body(splits, source_ref, sizes_ref, pair_ref, block_ref, row_ref, column_ref, own_ref, other_ref, *refs):
    out_ref = refs[-1]
    pairs = out_ref.shape[0]
    halves = refs[0].shape[2]
    share = pairs // halves
    inner = TILE // share
    own, core = place()
    shape = (TILE, TILE)
    row_live = lax.broadcasted_iota(jnp.int32, shape, 0) < sizes_ref[own * 2 + core]
    lane = lax.broadcasted_iota(jnp.int32, shape, 1)
    source = source_ref[pl.program_id(0)]

    def one(blocks):
        for rel, mine_ref in enumerate((own_ref, other_ref)):
            half = lax.rem(core + rel, 2)
            tile = source * 2 + half
            target = pl.ds(pl.multiple_of(half * TILE, TILE), TILE)
            live = row_live & (lane < sizes_ref[tile])
            energy = row_ref[...] + column_ref[half]

            def some_pairs(h, carry):
                for i in range(share):
                    p = h * share + i
                    theirs = jnp.concatenate(
                        [ref[r, rel, h, :, i * inner : (i + 1) * inner] for ref, r in blocks], axis=1
                    )
                    residual = mine_ref[p].astype(jnp.float32) + theirs.astype(jnp.float32)
                    block = jnp.where(live, block_ref[tile, p].astype(jnp.float32), 0.0)
                    scaled = residual * pl.reciprocal(energy - pair_ref[p])
                    out_ref[p, :, target] = (block * scaled).astype(jnp.bfloat16)
                return carry

            lax.fori_loop(0, halves, some_pairs, 0)

    first = 0
    for d, count in enumerate(splits):
        if count == 1:
            blocks = [(refs[first], r) for r in range(PARTS)]
        else:
            blocks = [(refs[first + r], 0) for r in range(PARTS)]
        pl.when(pl.program_id(0) == d)(functools.partial(one, blocks))
        first += count


def finish(sources, sizes, pair_energy, block_row, energy_row, energy_all, own, other, arrived, target):
    pairs, rows, columns = own.shape
    count = len(arrived)
    splits = tuple(len(blocks) for blocks in arrived)
    swapped = [block for blocks in arrived for block in blocks]
    smem = pl.BlockSpec(memory_space=pltpu.SMEM)
    own_spec = pl.BlockSpec((pairs, rows, TILE), lambda t, source: (0, 0, source[t]))
    before = 8 + len(swapped)
    return pl.pallas_call(
        functools.partial(finish_body, splits),
        out_shape=jax.ShapeDtypeStruct((pairs, rows, 2 * columns), jnp.bfloat16),
        grid_spec=pltpu.PrefetchScalarGridSpec(
            num_scalar_prefetch=1,
            grid=(count,),
            in_specs=[
                smem,
                smem,
                smem,
                pl.BlockSpec((rows, 1), lambda t, source: (0, 0)),
                pl.BlockSpec((2, 1, TILE), lambda t, source: (source[t], 0, 0)),
                own_spec,
                own_spec,
            ]
            + [pl.BlockSpec(block.shape, lambda t, source: (0, 0, 0, 0, 0)) for block in swapped]
            + ([] if target is None else [pl.BlockSpec(memory_space=pl.ANY)]),
            out_specs=pl.BlockSpec((pairs, rows, 2 * TILE), lambda t, source: (0, 0, source[t])),
        ),
        input_output_aliases={} if target is None else {before: 0},
        cost_estimate=pl.CostEstimate(
            flops=20 * count * pairs * rows * TILE,
            bytes_accessed=12 * count * pairs * rows * TILE,
            transcendentals=0,
        ),
        name="finish",
    )(
        sources,
        sizes,
        pair_energy,
        block_row,
        energy_row,
        energy_all,
        own,
        other,
        *swapped,
        *([] if target is None else [target]),
    )


def per_device(amplitudes, integrals, coupling, pair_energy, virtual_energy, tile_sizes, blocks):
    pairs, rows, _ = amplitudes.shape
    tiles = tile_sizes.shape[0]
    chips = tiles // 2
    wide_index = lax.axis_index("wide")
    perm_index = lax.axis_index("perm")
    coef = lax.dynamic_slice_in_dim(coupling, wide_index * pairs, pairs, 0)
    before = wide_shift(amplitudes, 1)
    after = wide_shift(amplitudes, -1)
    *kept_columns, given_columns = split(integrals)
    taken_columns = core_swap(given_columns)
    depth = 2 * rows // STREAMS
    moving = kept_columns + [taken_columns[start : start + depth] for start in range(0, rows, depth)]
    pieces = list(moving)
    for _ in range(1, chips):
        for i in range(STREAMS):
            moving[i] = mirrored(moving[i], 1)
        pieces += moving
    mixed, other = [], []
    for r in range(PARTS):
        kept_rows, given_rows = mix(r, coef, before, amplitudes, after)
        mixed.append(kept_rows)
        other.append(core_swap(given_rows))
    own, sent = [], []
    arrived = {d: [] for d in range(chips)}
    for r in range(PARTS):
        kept, given, *sent = product(r, mixed[r], other[r], pieces, own, sent)
        own = [kept, given]
        for d in EARLY:
            arrived[d].append(mirrored(sent[d], d))
    arrived[0].append(sent[0])
    for d in LATE:
        arrived[d].append(mirrored(sent[d], d))
    returned = core_swap(own[1])
    block_row = lax.dynamic_index_in_dim(blocks, perm_index, 1, keepdims=False).T
    energy_row = lax.dynamic_slice_in_dim(virtual_energy, perm_index * rows, rows, 0)[:, None]
    update = None
    for group in FINISH:
        back = jnp.array(group, jnp.int32)
        sources = (perm_index // 2 + jnp.where(perm_index % 2 == 0, chips - back, back)) % chips
        ready = [arrived[d] for d in group]
        update = finish(
            sources.astype(jnp.int32),
            tile_sizes,
            pair_energy,
            block_row,
            energy_row,
            virtual_energy.reshape(tiles, 1, TILE),
            own[0],
            returned,
            ready,
            update,
        )
    return update


def solution(mesh):
    in_specs = (
        P("wide", "perm", None),
        P("perm", None),
        P(),
        P("wide"),
        P(),
        P(),
        P("wide", None, None),
    )
    out_specs = P("wide", "perm", None)

    return jax.shard_map(
        per_device, mesh=mesh, in_specs=in_specs, out_specs=out_specs, check_vma=False
    )
```

```python
import functools

import jax
import jax.numpy as jnp
from jax import lax
from jax.experimental import pallas as pl
from jax.experimental.pallas import tpu as pltpu
from jax.sharding import PartitionSpec as P


TILE = 128
ALL_VMEM = pltpu.CompilerParams(vmem_limit_bytes=67_043_328)
PARTS = 2
STREAMS = 4
EARLY = (3, 4)
LATE = (5, 2, 6, 1, 7)
FINISH = ((0, 4, 3, 5), (2, 6, 1, 7))


def wide_shift(block, distance):
    size = lax.axis_size("wide")
    route = [(i, i + distance) for i in range(size) if 0 <= i + distance < size]
    return lax.ppermute(block, "wide", route)


def core_swap(block):
    size = lax.axis_size("perm")
    return lax.ppermute(block, "perm", [(i, i ^ 1) for i in range(size)])


def mirrored(block, distance):
    size = lax.axis_size("perm")
    chips = size // 2
    route = []
    for i in range(size):
        z, core = divmod(i, 2)
        route.append((i, (z + (distance if core == 0 else -distance)) % chips * 2 + core))
    return lax.ppermute(block, "perm", route)


def place():
    index = lax.axis_index("perm")
    return index // 2, lax.rem(index, 2)


def steps_from(z, chips, turn=0):
    own, core = place()
    core = lax.rem(core + turn, 2)
    ahead = lax.rem(own - z + chips, chips)
    return jnp.where(core == 0, ahead, lax.rem(chips - ahead, chips))


def mix_body(coef_ref, before_ref, own_ref, after_ref, *mixed_refs):
    pairs, rows, width = own_ref.shape
    taps = coef_ref.shape[0]
    first = lax.axis_index("wide") * pairs
    chips = width // TILE // 2
    step = 32

    def one_tile(t, carry):
        source = pl.ds(pl.multiple_of(t * TILE, TILE), TILE)
        targets = []
        for turn in range(2):
            dz = steps_from(t // 2, chips, turn)
            dc = lax.rem(t + place()[1] + turn, 2)
            targets.append(pl.ds(pl.multiple_of((dz * 2 + dc) * TILE, TILE), TILE))
        for start in range(0, rows, step):
            total = [None] * pairs
            for q in range(3 * pairs):
                ref = (before_ref, own_ref, after_ref)[q // pairs]
                value = ref[q % pairs, start : start + step, source].astype(jnp.float32)
                for p in range(pairs):
                    if 0 <= q - p < taps:
                        term = coef_ref[q - p, first + p] * value
                        total[p] = term if total[p] is None else total[p] + term
            for p in range(pairs):
                rounded = total[p].astype(jnp.bfloat16)
                for ref, target in zip(mixed_refs, targets):
                    ref[p, start : start + step, target] = rounded
        return carry

    lax.fori_loop(0, width // TILE, one_tile, 0)


def mix(which, coef, before, own, after):
    pairs, rows, width = own.shape
    rows = rows // PARTS
    step = 32
    smem = pl.BlockSpec(memory_space=pltpu.SMEM)
    skip = which * rows // step
    spec = pl.BlockSpec((pairs, step, width), lambda t: (0, skip + t, 0))
    return pl.pallas_call(
        mix_body,
        out_shape=[jax.ShapeDtypeStruct((pairs, rows, width), jnp.bfloat16)] * 2,
        grid=(rows // step,),
        in_specs=[smem, spec, spec, spec],
        out_specs=[pl.BlockSpec((pairs, step, width), lambda t: (0, t, 0))] * 2,
        cost_estimate=pl.CostEstimate(
            flops=18 * pairs * rows * width, bytes_accessed=8 * pairs * rows * width, transcendentals=0
        ),
        compiler_params=ALL_VMEM,
        name="mix",
    )(coef, before, own, after)


def split_body(in_ref, *refs):
    kept_refs, given_ref = refs[:-1], refs[-1]
    depth = kept_refs[0].shape[0]
    _, core = place()
    for z in range(given_ref.shape[1] // TILE):
        target = pl.ds(z * TILE, TILE)
        mine = pl.ds(pl.multiple_of((2 * z + core) * TILE, TILE), TILE)
        other = pl.ds(pl.multiple_of((2 * z + 1 - core) * TILE, TILE), TILE)
        given_ref[:, target] = in_ref[:, other]
        for i, ref in enumerate(kept_refs):
            ref[:, target] = in_ref[i * depth : (i + 1) * depth, mine]


def split(integrals):
    rows, width = integrals.shape
    depth = 2 * rows // STREAMS
    count = rows // depth
    vmem = pl.BlockSpec(memory_space=pltpu.VMEM)
    return pl.pallas_call(
        split_body,
        out_shape=[jax.ShapeDtypeStruct((depth, width // 2), jnp.bfloat16)] * count
        + [jax.ShapeDtypeStruct((rows, width // 2), jnp.bfloat16)],
        in_specs=[vmem],
        out_specs=[vmem] * (count + 1),
        cost_estimate=pl.CostEstimate(flops=0, bytes_accessed=4 * rows * width, transcendentals=0),
        name="split",
    )(integrals)


def product_body(count, chips, *refs):
    mixed_refs, pieces, outs = refs[:2], refs[2 : 2 + count], refs[-2 - chips :]
    own_refs, sent_refs = outs[:2], outs[2:]
    pairs, rows, width = mixed_refs[0].shape
    halves = sent_refs[0].shape[2]
    weights = jnp.concatenate([piece[...] for piece in pieces], axis=0)
    left = jnp.concatenate([ref[...].reshape(pairs * rows, width) for ref in mixed_refs], axis=0)
    result = jnp.dot(left, weights, preferred_element_type=jnp.float32).astype(jnp.bfloat16)
    for c in range(2):
        part = result[c * pairs * rows : (c + 1) * pairs * rows]
        own_refs[c][...] = part.reshape(pairs, rows, part.shape[1])
    turned = result.T
    group = result.shape[1] // TILE
    for i in range(group):
        z = pl.program_id(0) * group + i
        slot = lax.rem(chips - steps_from(z, chips), chips)

        def store(ref, i=i):
            for c in range(2):
                for h in range(halves):
                    start = (c * halves + h) * TILE
                    ref[0, c, h] = turned[i * TILE : (i + 1) * TILE, start : start + TILE]

        for d in range(chips):
            pl.when(slot == d)(functools.partial(store, sent_refs[d]))


def product(which, mixed, other, pieces, own_targets, sent_targets):
    pairs, rows, width = mixed.shape
    columns = pieces[0].shape[1]
    chips = columns // TILE
    wide = 2 * TILE
    halves = pairs * rows // TILE
    own = jax.ShapeDtypeStruct((pairs, PARTS * rows, columns), jnp.bfloat16)
    own_spec = pl.BlockSpec((pairs, rows, wide), lambda t: (0, which, t))
    inner = (2, halves, TILE, TILE)
    sent_shapes, sent_specs = [], []
    targets = list(own_targets)
    aliases = {2 + len(pieces) + i: i for i in range(len(targets))}
    for d in range(chips):
        apart = d in EARLY
        sent_shapes.append(jax.ShapeDtypeStruct((1 if apart else PARTS,) + inner, jnp.bfloat16))
        at = 0 if apart else which
        sent_specs.append(pl.BlockSpec((1,) + inner, lambda t, at=at: (at, 0, 0, 0, 0)))
        if sent_targets and not apart:
            aliases[2 + len(pieces) + len(targets)] = 2 + d
            targets.append(sent_targets[d])
    return pl.pallas_call(
        functools.partial(product_body, len(pieces), chips),
        out_shape=[own, own] + sent_shapes,
        grid=(columns // wide,),
        in_specs=[pl.BlockSpec((pairs, rows, width), lambda t: (0, 0, 0))] * 2
        + [pl.BlockSpec((piece.shape[0], wide), lambda t: (0, t)) for piece in pieces]
        + [pl.BlockSpec(memory_space=pl.ANY)] * len(targets),
        out_specs=[own_spec, own_spec] + sent_specs,
        input_output_aliases=aliases,
        cost_estimate=pl.CostEstimate(
            flops=4 * pairs * rows * width * columns,
            bytes_accessed=4 * pairs * rows * (width + columns) + 2 * width * columns,
            transcendentals=0,
        ),
        compiler_params=ALL_VMEM,
        name="product",
    )(mixed, other, *pieces, *targets)


def finish_body(splits, source_ref, sizes_ref, pair_ref, block_ref, row_ref, column_ref, own_ref, other_ref, *refs):
    out_ref = refs[-1]
    pairs = out_ref.shape[0]
    halves = refs[0].shape[2]
    share = pairs // halves
    inner = TILE // share
    own, core = place()
    shape = (TILE, TILE)
    row_live = lax.broadcasted_iota(jnp.int32, shape, 0) < sizes_ref[own * 2 + core]
    lane = lax.broadcasted_iota(jnp.int32, shape, 1)
    source = source_ref[pl.program_id(0)]

    def one(blocks):
        for rel, mine_ref in enumerate((own_ref, other_ref)):
            half = lax.rem(core + rel, 2)
            tile = source * 2 + half
            target = pl.ds(pl.multiple_of(half * TILE, TILE), TILE)
            live = row_live & (lane < sizes_ref[tile])
            energy = row_ref[...] + column_ref[half]

            def some_pairs(h, carry):
                for i in range(share):
                    p = h * share + i
                    theirs = jnp.concatenate(
                        [ref[r, rel, h, :, i * inner : (i + 1) * inner] for ref, r in blocks], axis=1
                    )
                    residual = mine_ref[p].astype(jnp.float32) + theirs.astype(jnp.float32)
                    block = jnp.where(live, block_ref[tile, p].astype(jnp.float32), 0.0)
                    scaled = residual * pl.reciprocal(energy - pair_ref[p])
                    out_ref[p, :, target] = (block * scaled).astype(jnp.bfloat16)
                return carry

            lax.fori_loop(0, halves, some_pairs, 0)

    first = 0
    for d, count in enumerate(splits):
        if count == 1:
            blocks = [(refs[first], r) for r in range(PARTS)]
        else:
            blocks = [(refs[first + r], 0) for r in range(PARTS)]
        pl.when(pl.program_id(0) == d)(functools.partial(one, blocks))
        first += count


def finish(sources, sizes, pair_energy, block_row, energy_row, energy_all, own, other, arrived, target):
    pairs, rows, columns = own.shape
    count = len(arrived)
    splits = tuple(len(blocks) for blocks in arrived)
    swapped = [block for blocks in arrived for block in blocks]
    smem = pl.BlockSpec(memory_space=pltpu.SMEM)
    own_spec = pl.BlockSpec((pairs, rows, TILE), lambda t, source: (0, 0, source[t]))
    before = 8 + len(swapped)
    return pl.pallas_call(
        functools.partial(finish_body, splits),
        out_shape=jax.ShapeDtypeStruct((pairs, rows, 2 * columns), jnp.bfloat16),
        grid_spec=pltpu.PrefetchScalarGridSpec(
            num_scalar_prefetch=1,
            grid=(count,),
            in_specs=[
                smem,
                smem,
                smem,
                pl.BlockSpec((rows, 1), lambda t, source: (0, 0)),
                pl.BlockSpec((2, 1, TILE), lambda t, source: (source[t], 0, 0)),
                own_spec,
                own_spec,
            ]
            + [pl.BlockSpec(block.shape, lambda t, source: (0, 0, 0, 0, 0)) for block in swapped]
            + ([] if target is None else [pl.BlockSpec(memory_space=pl.ANY)]),
            out_specs=pl.BlockSpec((pairs, rows, 2 * TILE), lambda t, source: (0, 0, source[t])),
        ),
        input_output_aliases={} if target is None else {before: 0},
        cost_estimate=pl.CostEstimate(
            flops=20 * count * pairs * rows * TILE,
            bytes_accessed=12 * count * pairs * rows * TILE,
            transcendentals=0,
        ),
        compiler_params=ALL_VMEM,
        name="finish",
    )(
        sources,
        sizes,
        pair_energy,
        block_row,
        energy_row,
        energy_all,
        own,
        other,
        *swapped,
        *([] if target is None else [target]),
    )


def per_device(amplitudes, integrals, coupling, pair_energy, virtual_energy, tile_sizes, blocks):
    _, rows, _ = amplitudes.shape
    tiles = tile_sizes.shape[0]
    chips = tiles // 2
    perm_index = lax.axis_index("perm")
    coef = coupling.T
    before = wide_shift(amplitudes, 1)
    after = wide_shift(amplitudes, -1)
    *kept_columns, given_columns = split(integrals)
    taken_columns = core_swap(given_columns)
    depth = 2 * rows // STREAMS
    moving = kept_columns + [taken_columns[start : start + depth] for start in range(0, rows, depth)]
    pieces = list(moving)
    for _ in range(1, chips):
        for i in range(STREAMS):
            moving[i] = mirrored(moving[i], 1)
        pieces += moving
    mixed, other = [], []
    for r in range(PARTS):
        kept_rows, given_rows = mix(r, coef, before, amplitudes, after)
        mixed.append(kept_rows)
        other.append(core_swap(given_rows))
    own, sent = [], []
    arrived = {d: [] for d in range(chips)}
    for r in range(PARTS):
        kept, given, *sent = product(r, mixed[r], other[r], pieces, own, sent)
        own = [kept, given]
        for d in EARLY:
            arrived[d].append(mirrored(sent[d], d))
    arrived[0].append(sent[0])
    for d in LATE:
        arrived[d].append(mirrored(sent[d], d))
    returned = core_swap(own[1])
    block_row = lax.dynamic_index_in_dim(blocks, perm_index, 1, keepdims=False).T
    energy_row = lax.dynamic_slice_in_dim(virtual_energy, perm_index * rows, rows, 0)[:, None]
    update = None
    for group in FINISH:
        back = jnp.array(group, jnp.int32)
        sources = (perm_index // 2 + jnp.where(perm_index % 2 == 0, chips - back, back)) % chips
        ready = [arrived[d] for d in group]
        update = finish(
            sources.astype(jnp.int32),
            tile_sizes,
            pair_energy,
            block_row,
            energy_row,
            virtual_energy.reshape(tiles, 1, TILE),
            own[0],
            returned,
            ready,
            update,
        )
    return update


def solution(mesh):
    in_specs = (
        P("wide", "perm", None),
        P("perm", None),
        P(),
        P("wide"),
        P(),
        P(),
        P("wide", None, None),
    )
    out_specs = P("wide", "perm", None)

    return jax.shard_map(
        per_device, mesh=mesh, in_specs=in_specs, out_specs=out_specs, check_vma=False
    )
```

```python
import functools

import jax
import jax.numpy as jnp
from jax import lax
from jax.experimental import pallas as pl
from jax.experimental.pallas import tpu as pltpu
from jax.sharding import PartitionSpec as P


TILE = 128
ALL_VMEM = pltpu.CompilerParams(vmem_limit_bytes=67_043_328)
PARTS = 2
STREAMS = 4
EARLY = (3, 4)
LATE = (5, 1, 7, 2, 6)
FINISH = ((0, 4, 3, 5), (2, 6, 1, 7))


def wide_shift(block, distance):
    size = lax.axis_size("wide")
    route = [(i, i + distance) for i in range(size) if 0 <= i + distance < size]
    return lax.ppermute(block, "wide", route)


def core_swap(block):
    size = lax.axis_size("perm")
    return lax.ppermute(block, "perm", [(i, i ^ 1) for i in range(size)])


def mirrored(block, distance):
    size = lax.axis_size("perm")
    chips = size // 2
    route = []
    for i in range(size):
        z, core = divmod(i, 2)
        route.append((i, (z + (distance if core == 0 else -distance)) % chips * 2 + core))
    return lax.ppermute(block, "perm", route)


def place():
    index = lax.axis_index("perm")
    return index // 2, lax.rem(index, 2)


def steps_from(z, chips, turn=0):
    own, core = place()
    core = lax.rem(core + turn, 2)
    ahead = lax.rem(own - z + chips, chips)
    return jnp.where(core == 0, ahead, lax.rem(chips - ahead, chips))


def mix_body(coef_ref, before_ref, own_ref, after_ref, *mixed_refs):
    pairs, rows, width = own_ref.shape
    taps = coef_ref.shape[0]
    first = lax.axis_index("wide") * pairs
    chips = width // TILE // 2
    step = 32

    def two_tiles(u, carry):
        sources, targets = [], []
        for i in range(2):
            t = 2 * u + i
            sources.append(pl.ds(pl.multiple_of(t * TILE, TILE), TILE))
            for turn in range(2):
                dz = steps_from(u, chips, turn)
                dc = lax.rem(i + place()[1] + turn, 2)
                targets.append(pl.ds(pl.multiple_of((dz * 2 + dc) * TILE, TILE), TILE))
        for start in range(0, rows, step):
            total = [[None, None] for _ in range(pairs)]
            for q in range(3 * pairs):
                ref = (before_ref, own_ref, after_ref)[q // pairs]
                values = [ref[q % pairs, start : start + step, at].astype(jnp.float32) for at in sources]
                for p in range(pairs):
                    if 0 <= q - p < taps:
                        weight = coef_ref[q - p, first + p]
                        for i in range(2):
                            term = weight * values[i]
                            total[p][i] = term if total[p][i] is None else total[p][i] + term
            for p in range(pairs):
                for i in range(2):
                    rounded = total[p][i].astype(jnp.bfloat16)
                    for turn in range(2):
                        mixed_refs[turn][p, start : start + step, targets[2 * i + turn]] = rounded
        return carry

    lax.fori_loop(0, width // TILE // 2, two_tiles, 0)


def mix(which, coef, before, own, after):
    pairs, rows, width = own.shape
    rows = rows // PARTS
    step = 32
    smem = pl.BlockSpec(memory_space=pltpu.SMEM)
    skip = which * rows // step
    spec = pl.BlockSpec((pairs, step, width), lambda t: (0, skip + t, 0))
    return pl.pallas_call(
        mix_body,
        out_shape=[jax.ShapeDtypeStruct((pairs, rows, width), jnp.bfloat16)] * 2,
        grid=(rows // step,),
        in_specs=[smem, spec, spec, spec],
        out_specs=[pl.BlockSpec((pairs, step, width), lambda t: (0, t, 0))] * 2,
        cost_estimate=pl.CostEstimate(
            flops=18 * pairs * rows * width, bytes_accessed=8 * pairs * rows * width, transcendentals=0
        ),
        compiler_params=ALL_VMEM,
        name="mix",
    )(coef, before, own, after)


def split_body(in_ref, *refs):
    kept_refs, given_ref = refs[:-1], refs[-1]
    depth = kept_refs[0].shape[0]
    _, core = place()
    for z in range(given_ref.shape[1] // TILE):
        target = pl.ds(z * TILE, TILE)
        mine = pl.ds(pl.multiple_of((2 * z + core) * TILE, TILE), TILE)
        other = pl.ds(pl.multiple_of((2 * z + 1 - core) * TILE, TILE), TILE)
        given_ref[:, target] = in_ref[:, other]
        for i, ref in enumerate(kept_refs):
            ref[:, target] = in_ref[i * depth : (i + 1) * depth, mine]


def split(integrals):
    rows, width = integrals.shape
    depth = 2 * rows // STREAMS
    count = rows // depth
    vmem = pl.BlockSpec(memory_space=pltpu.VMEM)
    return pl.pallas_call(
        split_body,
        out_shape=[jax.ShapeDtypeStruct((depth, width // 2), jnp.bfloat16)] * count
        + [jax.ShapeDtypeStruct((rows, width // 2), jnp.bfloat16)],
        in_specs=[vmem],
        out_specs=[vmem] * (count + 1),
        cost_estimate=pl.CostEstimate(flops=0, bytes_accessed=4 * rows * width, transcendentals=0),
        name="split",
    )(integrals)


def product_body(count, chips, *refs):
    mixed_refs, pieces, outs = refs[:2], refs[2 : 2 + count], refs[-2 - chips :]
    own_refs, sent_refs = outs[:2], outs[2:]
    pairs, rows, width = mixed_refs[0].shape
    halves = sent_refs[0].shape[2]
    weights = jnp.concatenate([piece[...] for piece in pieces], axis=0)
    left = jnp.concatenate([ref[...].reshape(pairs * rows, width) for ref in mixed_refs], axis=0)
    result = jnp.dot(left, weights, preferred_element_type=jnp.float32).astype(jnp.bfloat16)
    for c in range(2):
        part = result[c * pairs * rows : (c + 1) * pairs * rows]
        own_refs[c][...] = part.reshape(pairs, rows, part.shape[1])
    turned = result.T
    group = result.shape[1] // TILE
    for i in range(group):
        z = pl.program_id(0) * group + i
        slot = lax.rem(chips - steps_from(z, chips), chips)

        def store(ref, i=i):
            for c in range(2):
                for h in range(halves):
                    start = (c * halves + h) * TILE
                    ref[0, c, h] = turned[i * TILE : (i + 1) * TILE, start : start + TILE]

        for d in range(chips):
            pl.when(slot == d)(functools.partial(store, sent_refs[d]))


def product(which, mixed, other, pieces, own_targets, sent_targets):
    pairs, rows, width = mixed.shape
    columns = pieces[0].shape[1]
    chips = columns // TILE
    wide = 2 * TILE
    halves = pairs * rows // TILE
    own = jax.ShapeDtypeStruct((pairs, PARTS * rows, columns), jnp.bfloat16)
    own_spec = pl.BlockSpec((pairs, rows, wide), lambda t: (0, which, t))
    inner = (2, halves, TILE, TILE)
    sent_shapes, sent_specs = [], []
    targets = list(own_targets)
    aliases = {2 + len(pieces) + i: i for i in range(len(targets))}
    for d in range(chips):
        apart = d in EARLY
        sent_shapes.append(jax.ShapeDtypeStruct((1 if apart else PARTS,) + inner, jnp.bfloat16))
        at = 0 if apart else which
        sent_specs.append(pl.BlockSpec((1,) + inner, lambda t, at=at: (at, 0, 0, 0, 0)))
        if sent_targets and not apart:
            aliases[2 + len(pieces) + len(targets)] = 2 + d
            targets.append(sent_targets[d])
    return pl.pallas_call(
        functools.partial(product_body, len(pieces), chips),
        out_shape=[own, own] + sent_shapes,
        grid=(columns // wide,),
        in_specs=[pl.BlockSpec((pairs, rows, width), lambda t: (0, 0, 0))] * 2
        + [pl.BlockSpec((piece.shape[0], wide), lambda t: (0, t)) for piece in pieces]
        + [pl.BlockSpec(memory_space=pl.ANY)] * len(targets),
        out_specs=[own_spec, own_spec] + sent_specs,
        input_output_aliases=aliases,
        cost_estimate=pl.CostEstimate(
            flops=4 * pairs * rows * width * columns,
            bytes_accessed=4 * pairs * rows * (width + columns) + 2 * width * columns,
            transcendentals=0,
        ),
        compiler_params=ALL_VMEM,
        name="product",
    )(mixed, other, *pieces, *targets)


def finish_body(splits, source_ref, sizes_ref, pair_ref, block_ref, row_ref, column_ref, own_ref, other_ref, *refs):
    out_ref = refs[-1]
    pairs = out_ref.shape[0]
    halves = refs[0].shape[2]
    share = pairs // halves
    inner = TILE // share
    own, core = place()
    shape = (TILE, TILE)
    row_live = lax.broadcasted_iota(jnp.int32, shape, 0) < sizes_ref[own * 2 + core]
    lane = lax.broadcasted_iota(jnp.int32, shape, 1)
    source = source_ref[pl.program_id(0)]

    def one(blocks):
        for rel, mine_ref in enumerate((own_ref, other_ref)):
            half = lax.rem(core + rel, 2)
            tile = source * 2 + half
            target = pl.ds(pl.multiple_of(half * TILE, TILE), TILE)
            live = row_live & (lane < sizes_ref[tile])
            energy = row_ref[...] + column_ref[half]

            def some_pairs(h, carry):
                for i in range(share):
                    p = h * share + i
                    theirs = jnp.concatenate(
                        [ref[r, rel, h, :, i * inner : (i + 1) * inner] for ref, r in blocks], axis=1
                    )
                    residual = mine_ref[p].astype(jnp.float32) + theirs.astype(jnp.float32)
                    block = jnp.where(live, block_ref[tile, p].astype(jnp.float32), 0.0)
                    scaled = residual * pl.reciprocal(energy - pair_ref[p])
                    out_ref[p, :, target] = (block * scaled).astype(jnp.bfloat16)
                return carry

            lax.fori_loop(0, halves, some_pairs, 0)

    first = 0
    for d, count in enumerate(splits):
        if count == 1:
            blocks = [(refs[first], r) for r in range(PARTS)]
        else:
            blocks = [(refs[first + r], 0) for r in range(PARTS)]
        pl.when(pl.program_id(0) == d)(functools.partial(one, blocks))
        first += count


def finish(sources, sizes, pair_energy, block_row, energy_row, energy_all, own, other, arrived, target):
    pairs, rows, columns = own.shape
    count = len(arrived)
    splits = tuple(len(blocks) for blocks in arrived)
    swapped = [block for blocks in arrived for block in blocks]
    smem = pl.BlockSpec(memory_space=pltpu.SMEM)
    own_spec = pl.BlockSpec((pairs, rows, TILE), lambda t, source: (0, 0, source[t]))
    before = 8 + len(swapped)
    return pl.pallas_call(
        functools.partial(finish_body, splits),
        out_shape=jax.ShapeDtypeStruct((pairs, rows, 2 * columns), jnp.bfloat16),
        grid_spec=pltpu.PrefetchScalarGridSpec(
            num_scalar_prefetch=1,
            grid=(count,),
            in_specs=[
                smem,
                smem,
                smem,
                pl.BlockSpec((rows, 1), lambda t, source: (0, 0)),
                pl.BlockSpec((2, 1, TILE), lambda t, source: (source[t], 0, 0)),
                own_spec,
                own_spec,
            ]
            + [pl.BlockSpec(block.shape, lambda t, source: (0, 0, 0, 0, 0)) for block in swapped]
            + ([] if target is None else [pl.BlockSpec(memory_space=pl.ANY)]),
            out_specs=pl.BlockSpec((pairs, rows, 2 * TILE), lambda t, source: (0, 0, source[t])),
        ),
        input_output_aliases={} if target is None else {before: 0},
        cost_estimate=pl.CostEstimate(
            flops=20 * count * pairs * rows * TILE,
            bytes_accessed=12 * count * pairs * rows * TILE,
            transcendentals=0,
        ),
        compiler_params=ALL_VMEM,
        name="finish",
    )(
        sources,
        sizes,
        pair_energy,
        block_row,
        energy_row,
        energy_all,
        own,
        other,
        *swapped,
        *([] if target is None else [target]),
    )


def per_device(amplitudes, integrals, coupling, pair_energy, virtual_energy, tile_sizes, blocks):
    _, rows, _ = amplitudes.shape
    tiles = tile_sizes.shape[0]
    chips = tiles // 2
    perm_index = lax.axis_index("perm")
    coef = coupling.T
    before = wide_shift(amplitudes, 1)
    after = wide_shift(amplitudes, -1)
    *kept_columns, given_columns = split(integrals)
    taken_columns = core_swap(given_columns)
    depth = 2 * rows // STREAMS
    moving = kept_columns + [taken_columns[start : start + depth] for start in range(0, rows, depth)]
    pieces = list(moving)
    for _ in range(1, chips):
        for i in range(STREAMS):
            moving[i] = mirrored(moving[i], 1)
        pieces += moving
    mixed, other = [], []
    for r in range(PARTS):
        kept_rows, given_rows = mix(r, coef, before, amplitudes, after)
        mixed.append(kept_rows)
        other.append(core_swap(given_rows))
    own, sent = [], []
    arrived = {d: [] for d in range(chips)}
    for r in range(PARTS):
        kept, given, *sent = product(r, mixed[r], other[r], pieces, own, sent)
        own = [kept, given]
        for d in EARLY:
            arrived[d].append(mirrored(sent[d], d))
    arrived[0].append(sent[0])
    for d in LATE:
        arrived[d].append(mirrored(sent[d], d))
    returned = core_swap(own[1])
    block_row = lax.dynamic_index_in_dim(blocks, perm_index, 1, keepdims=False).T
    energy_row = lax.dynamic_slice_in_dim(virtual_energy, perm_index * rows, rows, 0)[:, None]
    update = None
    for group in FINISH:
        back = jnp.array(group, jnp.int32)
        sources = (perm_index // 2 + jnp.where(perm_index % 2 == 0, chips - back, back)) % chips
        ready = [arrived[d] for d in group]
        update = finish(
            sources.astype(jnp.int32),
            tile_sizes,
            pair_energy,
            block_row,
            energy_row,
            virtual_energy.reshape(tiles, 1, TILE),
            own[0],
            returned,
            ready,
            update,
        )
    return update


def solution(mesh):
    in_specs = (
        P("wide", "perm", None),
        P("perm", None),
        P(),
        P("wide"),
        P(),
        P(),
        P("wide", None, None),
    )
    out_specs = P("wide", "perm", None)

    return jax.shard_map(
        per_device, mesh=mesh, in_specs=in_specs, out_specs=out_specs, check_vma=False
    )
```
